32 devices in a mesh: dp: 4 (over z), dom: 8 (over y, x, core).
Axes of the slice: x: 2, y: 2, z: 4, core: 2. Of those that a mesh axis runs over, the one named last changes fastest.
Arguments:
- feats: bfloat16 [4096, 1024], P(('dp', 'dom')), parts along dimension 0, may hold values from -26 to 26
- adj_own: int32 [4096, 128], P(('dp', 'dom')), parts along dimension 0, may hold values 0 or 1
- adj_prev: int32 [4096, 32], P(('dp', 'dom')), parts along dimension 0, may hold values 0 or 1
- adj_next: int32 [4096, 32], P(('dp', 'dom')), parts along dimension 0, may hold values 0 or 1
- bcount: int32 [32, 2], P('dp'), parts along dimension 0, may hold values from 1 to 32
- wqkv: bfloat16 [3, 1024, 1024], P(None, None, 'dom'), may hold values from -1 to 1, as said below
- w_mp: bfloat16 [1024, 1024], P('dom'), may hold values from -0.1875 to 0.1875
- w_out: bfloat16 [1024, 1024], P('dom'), may hold values from -0.1875 to 0.1875
Outputs:
- updated: bfloat16 [4096, 1024], P(('dp', 'dom')), parts along dimension 0
The draws below stay inside these ranges and needn't reach their ends.
There are 4 independent parts, one for each index of `dp`. The reference program is written for one: setup_inputs(seed, part) draws one part's arguments, and reference() takes and returns one part's arrays. A program takes and returns all parts, laid end to end along the dimension named above; an argument that names none is the same for every part. Nothing has to cross between parts.
Inputs may be any that keep to these rules, and one draw needn't show every extreme that they name: `wqkv`: projection weights with entries of deviation about 1024 ** -0.5.
All inputs are finite; a program needn't handle non-finite values. No bound on the sum of `adj_own` or of `adj_prev` or of `adj_next` on one device may be relied on, other than what follows from the above.
Results may differ from the reference program's by a relative error of at most 0.0066.
Values may be sent and summed in bfloat16 or wider, within the bound.
A program may use at most 64 MiB of HBM per device.

```python
import jax
import jax.numpy as jnp
from jax import lax

D = 1024
HEADS = 32
NODE_DEV = 128
BND = 32
NODES = 1024
N_DOM = 8


def draw_feats(key, part):
    first = jax.random.fold_in(key, 0)
    base = jnp.clip(jax.random.normal(first, (NODES, D), jnp.float32), -5.0, 5.0)
    return base.astype(jnp.bfloat16)


def draw_wqkv(key, part):
    base = jnp.clip(jax.random.normal(key, (3, D, D), jnp.float32), -4.0, 4.0) / D ** 0.5
    return base.astype(jnp.bfloat16)


def set_ends(result, key, smallest, high):
    place = [jax.random.randint(jax.random.fold_in(key, axis), (), 0, length) for axis, length in enumerate(result.shape)]
    longest = result.shape.index(max(result.shape))
    next_to = place[:longest] + [(place[longest] + 1) % result.shape[longest]] + place[longest + 1:]
    return result.at[tuple(place)].set(smallest).at[tuple(next_to)].set(high)


def levels(key, dims, cuts, smallest, high):
    loudness = 1.0
    for dim, parts in cuts:
        steps = jax.random.uniform(jax.random.fold_in(jax.random.fold_in(key, 6), dim), (parts,), jnp.float32, smallest / len(cuts), high / len(cuts))
        loudness = loudness * jnp.repeat(jnp.exp(steps), dims[dim] // parts).reshape((-1,) + (1,) * (len(dims) - 1 - dim))
    return loudness


def scatter_about(rng, shape, deviation, reach, cuts=(), kind=jnp.bfloat16):
    drawn = deviation * jax.random.normal(rng, shape, jnp.float32)
    if cuts:
        drawn = drawn * levels(rng, shape, cuts, -0.22, 0.18)
    return jnp.clip(drawn, -reach, reach).astype(kind)


def setup_inputs(seed: int = 0, part: int = 0) -> dict:
    streams_of = jax.random.split(jax.random.key(seed), 9)
    own_keys = jax.random.split(jax.random.fold_in(streams_of[8], part), 9)
    feats = draw_feats(jax.random.fold_in(jax.random.fold_in(streams_of[8], part), 71), part)
    adj_own = set_ends((jax.random.randint(own_keys[1], (NODES, NODE_DEV), 0, 24) < 1).astype(jnp.int32), jax.random.fold_in(own_keys[1], 1), 0, 1)
    adj_prev = set_ends((jax.random.randint(own_keys[2], (NODES, BND), 0, 6) < 1).astype(jnp.int32), jax.random.fold_in(own_keys[2], 1), 0, 1)
    adj_next = set_ends((jax.random.randint(own_keys[3], (NODES, BND), 0, 6) < 1).astype(jnp.int32), jax.random.fold_in(own_keys[3], 1), 0, 1)
    bcount = set_ends(jax.random.randint(own_keys[4], (N_DOM, 2), 1, BND + 1), jax.random.fold_in(own_keys[4], 1), 1, BND).astype(jnp.int32)
    wqkv = draw_wqkv(jax.random.fold_in(streams_of[8], 71), part)
    w_mp = scatter_about(streams_of[6], (D, D), D ** -0.5, 0.1875, ((0, 8),))
    w_out = scatter_about(streams_of[7], (D, D), D ** -0.5, 0.1875, ((0, 8),))
    return dict(feats=feats, adj_own=adj_own, adj_prev=adj_prev, adj_next=adj_next, bcount=bcount, wqkv=wqkv, w_mp=w_mp, w_out=w_out)


def reference(feats, adj_own, adj_prev, adj_next, bcount, wqkv, w_mp, w_out):
    rows = NODE_DEV
    feat_parts = feats.reshape(N_DOM, rows, D)
    zero_rim = jnp.zeros((1, BND, D), feats.dtype)
    prev_rim = jnp.concatenate([zero_rim, feat_parts[:-1, rows - BND:]], 0)
    next_rim = jnp.concatenate([feat_parts[1:, :BND], zero_rim], 0)
    part_ids = jnp.arange(N_DOM).astype(jnp.int32)[:, None]
    column = jnp.arange(BND).astype(jnp.int32)[None, :]
    prev_count = jnp.concatenate([jnp.zeros((1,), jnp.int32), bcount[:-1, 1]])
    next_count = jnp.concatenate([bcount[1:, 0], jnp.zeros((1,), jnp.int32)])
    prev_vis = (part_ids > 0) & (column >= BND - prev_count[:, None])
    next_vis = (part_ids < N_DOM - 1) & (column < next_count[:, None])
    own = adj_own.reshape(N_DOM, rows, rows).astype(jnp.float32)
    prv = jnp.where(prev_vis[:, None, :], adj_prev.reshape(N_DOM, rows, BND), 0).astype(jnp.float32)
    nxt = jnp.where(next_vis[:, None, :], adj_next.reshape(N_DOM, rows, BND), 0).astype(jnp.float32)
    degree = 1.0 + jnp.sum(own, -1) + jnp.sum(prv, -1) + jnp.sum(nxt, -1)
    total = feat_parts.astype(jnp.float32)
    total = total + jnp.einsum("prc,pcd->prd", own, feat_parts.astype(jnp.float32))
    total = total + jnp.einsum("prc,pcd->prd", prv, prev_rim.astype(jnp.float32))
    total = total + jnp.einsum("prc,pcd->prd", nxt, next_rim.astype(jnp.float32))
    mixed = (total / degree[..., None]).astype(jnp.bfloat16).reshape(NODES, D)
    local = jnp.dot(mixed, w_mp, preferred_element_type=jnp.float32)
    query = jnp.dot(feats, wqkv[0], preferred_element_type=jnp.float32).astype(jnp.bfloat16)
    key = jnp.dot(feats, wqkv[1], preferred_element_type=jnp.float32).astype(jnp.bfloat16)
    value = jnp.dot(feats, wqkv[2], preferred_element_type=jnp.float32).astype(jnp.bfloat16)
    head_size = D // HEADS
    scale = 1.0 / (head_size ** 0.5)

    def split_heads(array):
        return array.reshape(NODES, HEADS, head_size).transpose(1, 0, 2)

    def one_head(items):
        q_head, k_head, v_head = items
        score = jnp.dot(q_head, k_head.T, preferred_element_type=jnp.float32) * scale
        peak = jnp.max(score, -1, keepdims=True)
        expo = jnp.exp(score - peak)
        weight = (expo / jnp.sum(expo, -1, keepdims=True)).astype(jnp.bfloat16)
        return jnp.dot(weight, v_head, preferred_element_type=jnp.float32).astype(jnp.bfloat16)

    per_head = lax.map(one_head, (split_heads(query), split_heads(key), split_heads(value)))
    heads_out = per_head.transpose(1, 0, 2).reshape(NODES, D)
    attn = jnp.dot(heads_out, w_out, preferred_element_type=jnp.float32)
    return (feats.astype(jnp.float32) + local + attn).astype(jnp.bfloat16)
```

```python
import functools
import math

import jax
import jax.numpy as jnp
from jax import lax
from jax.experimental import pallas as pl
from jax.experimental.pallas import tpu as pltpu
from jax.sharding import PartitionSpec as P

HEADS = 32


def with_halo(cells, sides, width):
    for axis, dim in sides:
        count = lax.axis_size(axis)
        ends = count - 1
        head = lax.slice_in_dim(cells, 0, width, axis=dim)
        tail = lax.slice_in_dim(cells, cells.shape[dim] - width, cells.shape[dim], axis=dim)
        cells = jnp.concatenate(
            [
                lax.ppermute(tail, axis, [(i, (i + 1) % count) for i in range(ends)]),
                cells,
                lax.ppermute(head, axis, [((i + 1) % count, i) for i in range(ends)]),
            ],
            axis=dim,
        )
    return cells


def attend(head_qkv, head_size):
    nodes = head_qkv.shape[1]
    columns = head_qkv.shape[2]
    count_heads = columns // head_size
    query = head_qkv[0].reshape(nodes, count_heads, head_size)
    key = head_qkv[1].reshape(nodes, count_heads, head_size)
    value = head_qkv[2].reshape(nodes, count_heads, head_size)
    scale = 1.0 / head_size**0.5
    block = math.gcd(nodes, 512)

    def one_block(index):
        q_block = lax.dynamic_slice_in_dim(query, index * block, block, 0)
        score = jnp.einsum("qhc,khc->hqk", q_block, key, preferred_element_type=jnp.float32) * scale
        peak = jnp.max(score, -1, keepdims=True)
        expo = jnp.exp(score - peak)
        weight = (expo / jnp.sum(expo, -1, keepdims=True)).astype(jnp.bfloat16)
        result = jnp.einsum("hqk,khc->qhc", weight, value, preferred_element_type=jnp.float32)
        return result.astype(jnp.bfloat16).reshape(block, columns)

    blocks = lax.map(one_block, jnp.arange(nodes // block))
    return blocks.reshape(nodes, columns)


def message_term(mixed, w_mp):
    return jnp.dot(
        mixed, lax.all_gather(w_mp, "dom", axis=0, tiled=True), preferred_element_type=jnp.float32
    )


def body(feats, adj_own, adj_prev, adj_next, bcount, wqkv, w_mp, w_out):
    rows = feats.shape[0]
    width = feats.shape[1]
    band = adj_prev.shape[1]
    parts = lax.axis_size("dom")
    myself = lax.axis_index("dom")
    padded = with_halo(feats, (("dom", 0),), band)
    prev_rim = padded[:band]
    next_rim = padded[band + rows :]
    column = jnp.arange(band)
    prev_count = bcount[jnp.maximum(myself - 1, 0), 1]
    next_count = bcount[jnp.minimum(myself + 1, parts - 1), 0]
    prev_vis = (myself > 0) & (column >= band - prev_count)
    next_vis = (myself < parts - 1) & (column < next_count)
    own = adj_own.astype(jnp.bfloat16)
    prv = jnp.where(prev_vis[None, :], adj_prev, 0).astype(jnp.bfloat16)
    nxt = jnp.where(next_vis[None, :], adj_next, 0).astype(jnp.bfloat16)
    degree = (
        1.0
        + jnp.sum(own.astype(jnp.float32), -1)
        + jnp.sum(prv.astype(jnp.float32), -1)
        + jnp.sum(nxt.astype(jnp.float32), -1)
    )
    total = feats.astype(jnp.float32) + jnp.dot(own, feats, preferred_element_type=jnp.float32)
    total = total + jnp.dot(prv, prev_rim, preferred_element_type=jnp.float32)
    total = total + jnp.dot(nxt, next_rim, preferred_element_type=jnp.float32)
    mixed = (total / degree[:, None]).astype(jnp.bfloat16)
    node_qkv = jnp.einsum(
        "nd,tdc->tnc",
        feats,
        lax.all_gather(wqkv, "dom", axis=2, tiled=True),
        preferred_element_type=jnp.float32,
    ).astype(jnp.bfloat16)
    head_qkv = lax.all_to_all(node_qkv, "dom", split_axis=2, concat_axis=1, tiled=True)
    head_out = attend(head_qkv, width // HEADS)
    node_out = lax.all_to_all(head_out, "dom", split_axis=0, concat_axis=1, tiled=True)
    local = message_term(mixed, w_mp)
    attn = jnp.dot(
        node_out,
        lax.all_gather(w_out, "dom", axis=0, tiled=True),
        preferred_element_type=jnp.float32,
    )
    return (feats.astype(jnp.float32) + local + attn).astype(jnp.bfloat16)


def layer_kernel(
    parts, head_size,
    feats, adj_own, adj_prev, adj_next, bcount, wqkv, w_mp, w_out, out,
    fall, wcat, w2, qs, kt, v1, ms, mr, lhs, keep, sib_out, sib_in, rs_out, rs_in,
    ag_send, ag_recv, mx_send, mx_recv, sb_send, sb_recv, rs_send, rs_recv,
):
    rows, width = feats.shape
    cols = w_out.shape[0]
    band = adj_prev.shape[1]
    half = rows // 2
    pair = 2 * rows
    heads = cols // head_size
    me = lax.axis_index("dom")
    core = me % 2
    chip = me // 2
    sib = me + 1 - 2 * core
    cx, cy = chip % 2, chip // 2

    def chip_at(dx, dy):
        return ((cy + dy) % 2) * 2 + (cx + dx) % 2

    x_chip, y_chip, d_chip = chip_at(1, 0), chip_at(0, 1), chip_at(1, 1)
    x_dev, y_dev, d_dev = x_chip * 2 + core, y_chip * 2 + core, d_chip * 2 + core
    mesh_id = pl.DeviceIdType.MESH

    def remote(src, dst, send_sem, recv_sem, dev):
        return pltpu.make_async_remote_copy(
            src_ref=src, dst_ref=dst, send_sem=send_sem, recv_sem=recv_sem,
            device_id={"dom": dev}, device_id_type=mesh_id,
        )

    barrier = pltpu.get_barrier_semaphore()
    for k in range(1, parts):
        pl.semaphore_signal(barrier, inc=1, device_id={"dom": (me + k) % parts}, device_id_type=mesh_id)
    pl.semaphore_wait(barrier, parts - 1)

    started = []

    def send_half(block, h, dev, own=False):
        span = pl.ds(half * h, half)
        dst = fall.at[block, span]
        src = feats.at[span] if own else dst
        copy = remote(src, dst, ag_send.at[len(started)], ag_recv.at[block, h], dev)
        copy.start()
        started.append(copy)

    def wait_half(block, h):
        dst = fall.at[block, pl.ds(half * h, half)]
        remote(dst, dst, ag_send.at[0], ag_recv.at[block, h], sib).wait_recv()

    send_half(me, 0, x_dev, True)
    send_half(me, 1, y_dev, True)
    send_half(me, 0, sib, True)
    send_half(me, 1, sib, True)
    send_half(me, 1, x_dev, True)
    send_half(me, 0, y_dev, True)

    fall[me] = feats[...]
    for t in range(3):
        wcat[:, t * cols : (t + 1) * cols] = wqkv[t]
    w2[:cols] = w_out[...]
    w2[cols:] = w_mp[...]
    v1[:, cols:] = jnp.ones_like(v1[:, cols:])
    lane_head = lax.broadcasted_iota(jnp.int32, (1, cols), 1) // head_size
    factor = math.log2(math.e) / head_size**0.5

    def project(c):
        base = pl.multiple_of(c * pair, pair)
        block = fall[pl.ds(2 * c, 2)].reshape(pair, width)
        r = jnp.dot(block, wcat[...], preferred_element_type=jnp.float32)
        q = r[:, :cols] * factor
        for h in range(heads):
            qs[h, pl.ds(base, pair), :] = jnp.where(lane_head == h, q, 0.0).astype(jnp.bfloat16)
        kt[:, pl.ds(base, pair)] = r[:, cols : 2 * cols].T.astype(jnp.bfloat16)
        v1[pl.ds(base, pair), :cols] = r[:, 2 * cols :].astype(jnp.bfloat16)

    def wait_sib(c):
        for h in range(2):
            wait_half(2 * c + 1 - core, h)

    wait_sib(chip)
    project(chip)
    wait_half(x_dev, 0)
    send_half(x_dev, 0, y_dev)
    send_half(x_dev, 0, sib)
    wait_half(y_dev, 1)
    send_half(y_dev, 1, x_dev)
    send_half(y_dev, 1, sib)
    wait_half(x_dev, 1)
    send_half(x_dev, 1, sib)
    wait_half(y_dev, 0)
    send_half(y_dev, 0, sib)
    wait_sib(x_chip)
    project(x_chip)
    wait_half(d_dev, 0)
    send_half(d_dev, 0, sib)
    wait_half(d_dev, 1)
    send_half(d_dev, 1, sib)
    wait_sib(y_chip)
    project(y_chip)
    wait_sib(d_chip)

    before, after = (me + parts - 1) % parts, (me + 1) % parts
    column = lax.broadcasted_iota(jnp.int32, (1, band), 1)
    prev_count = jnp.where(me > 0, bcount[before, 1], 0)
    next_count = jnp.where(me < parts - 1, bcount[after, 0], 0)
    own = adj_own[...].astype(jnp.float32)
    prv = jnp.where(column >= band - prev_count, adj_prev[...], 0).astype(jnp.float32)
    nxt = jnp.where(column < next_count, adj_next[...], 0).astype(jnp.float32)
    degree = (
        1.0
        + jnp.sum(own, -1, keepdims=True)
        + jnp.sum(prv, -1, keepdims=True)
        + jnp.sum(nxt, -1, keepdims=True)
    )
    total = feats[...].astype(jnp.float32)
    total += jnp.dot(own.astype(jnp.bfloat16), feats[...], preferred_element_type=jnp.float32)
    total += jnp.dot(
        prv.astype(jnp.bfloat16), fall[before, rows - band :, :], preferred_element_type=jnp.float32
    )
    total += jnp.dot(
        nxt.astype(jnp.bfloat16), fall[after, :band, :], preferred_element_type=jnp.float32
    )
    mixed = (total / degree).astype(jnp.bfloat16)
    for j in range(parts):
        ms[j] = mixed[:, j * cols : (j + 1) * cols]
    mix_copies = []
    for k in range(1, parts):
        to = (me + k) % parts
        copy = remote(ms.at[to], mr.at[me], mx_send.at[k], mx_recv.at[me], to)
        copy.start()
        mix_copies.append(copy)
    mr[me] = ms[me]
    project(d_chip)

    def attention(c):
        base = pl.multiple_of(c * pair, pair)
        result = jnp.zeros((pair, cols), jnp.float32)
        for h in range(heads):
            score = jnp.dot(
                qs[h, pl.ds(base, pair), :], kt[...], preferred_element_type=jnp.float32
            )
            peak = jnp.max(score, -1, keepdims=True)
            weight = jnp.exp2(score - peak).astype(jnp.bfloat16)
            both = jnp.dot(weight, v1[...], preferred_element_type=jnp.float32)
            result = jnp.where(lane_head == h, both[:, :cols] / both[:, cols:], result)
        lhs[:, :, :cols] = result.astype(jnp.bfloat16).reshape(2, rows, cols)

    def partial_sums(slot, c):
        lhs[:, :, cols:] = mr[pl.ds(2 * c, 2)]
        sib_out[slot] = jnp.dot(
            lhs[1 - core], w2[...], preferred_element_type=jnp.float32
        ).astype(jnp.bfloat16)
        to_sib(slot).start()
        keep[slot] = jnp.dot(lhs[core], w2[...], preferred_element_type=jnp.float32)

    def to_sib(slot):
        return remote(sib_out.at[slot], sib_in.at[slot], sb_send.at[slot], sb_recv.at[slot], sib)

    def to_chip(slot):
        c = chip_at((slot + 1) % 2, (slot + 1) // 2)
        return remote(
            rs_out.at[slot], rs_in.at[slot], rs_send.at[slot], rs_recv.at[slot], c * 2 + core
        )

    def combine(slot):
        to_sib(slot).wait_recv()
        rs_out[slot] = (keep[slot] + sib_in[slot].astype(jnp.float32)).astype(jnp.bfloat16)
        to_chip(slot).start()

    attention(d_chip)
    for k in range(1, parts):
        source = (me + k) % parts
        remote(ms.at[source], mr.at[source], mx_send.at[0], mx_recv.at[source], sib).wait_recv()
    partial_sums(2, d_chip)

    def step(i, _):
        slot = 1 - i
        c = chip_at((slot + 1) % 2, (slot + 1) // 2)
        attention(c)
        combine(slot + 1)
        partial_sums(slot, c)
        return 0

    lax.fori_loop(0, 2, step, 0)
    attention(chip)
    combine(0)
    partial_sums(3, chip)
    final = feats[...].astype(jnp.float32) + keep[3]
    to_sib(3).wait_recv()
    final += sib_in[3].astype(jnp.float32)
    for slot in (2, 1, 0):
        to_chip(slot).wait_recv()
        final += rs_in[slot].astype(jnp.float32)
    out[...] = final.astype(out.dtype)
    for copy in started:
        copy.wait_send()
    for copy in mix_copies:
        copy.wait_send()
    for slot in range(4):
        to_sib(slot).wait_send()
    for slot in range(3):
        to_chip(slot).wait_send()


def fused_layer(feats, adj_own, adj_prev, adj_next, bcount, wqkv, w_mp, w_out):
    rows, width = feats.shape
    cols = w_out.shape[0]
    parts = lax.axis_size("dom")
    nodes = rows * parts
    head_size = width // HEADS
    heads = cols // head_size
    vmem = pl.BlockSpec(memory_space=pltpu.VMEM)
    smem = pl.BlockSpec(memory_space=pltpu.SMEM)
    bf16, f32 = jnp.bfloat16, jnp.float32
    dma = pltpu.SemaphoreType.DMA
    return pl.pallas_call(
        functools.partial(layer_kernel, parts, head_size),
        out_shape=jax.ShapeDtypeStruct((rows, width), bf16),
        in_specs=[vmem, vmem, vmem, vmem, smem, vmem, vmem, vmem],
        out_specs=vmem,
        scratch_shapes=[
            pltpu.VMEM((parts, rows, width), bf16),
            pltpu.VMEM((width, 3 * cols), bf16),
            pltpu.VMEM((2 * cols, width), bf16),
            pltpu.VMEM((heads, nodes, cols), bf16),
            pltpu.VMEM((cols, nodes), bf16),
            pltpu.VMEM((nodes, 2 * cols), bf16),
            pltpu.VMEM((parts, rows, cols), bf16),
            pltpu.VMEM((parts, rows, cols), bf16),
            pltpu.VMEM((2, rows, 2 * cols), bf16),
            pltpu.VMEM((4, rows, width), f32),
            pltpu.VMEM((4, rows, width), bf16),
            pltpu.VMEM((4, rows, width), bf16),
            pltpu.VMEM((3, rows, width), bf16),
            pltpu.VMEM((3, rows, width), bf16),
            dma((14,)),
            dma((parts, 2)),
            dma((parts,)),
            dma((parts,)),
            dma((4,)),
            dma((4,)),
            dma((3,)),
            dma((3,)),
        ],
        compiler_params=pltpu.CompilerParams(
            collective_id=0, has_side_effects=True, vmem_limit_bytes=48 * 1024 * 1024
        ),
    )(feats, adj_own, adj_prev, adj_next, bcount, wqkv, w_mp, w_out)


def solution(mesh):
    placed = (
        P(("dp", "dom"), None),
        P(("dp", "dom"), None),
        P(("dp", "dom"), None),
        P(("dp", "dom"), None),
        P("dp", None),
        P(None, None, "dom"),
        P("dom", None),
        P("dom", None),
    )
    layer = fused_layer if mesh.shape["dom"] == 8 else body
    return jax.shard_map(
        layer, mesh=mesh, in_specs=placed, out_specs=P(("dp", "dom"), None), check_vma=False
    )
```

```python
import functools
import math

import jax
import jax.numpy as jnp
from jax import lax
from jax.experimental import pallas as pl
from jax.experimental.pallas import tpu as pltpu
from jax.sharding import PartitionSpec as P

HEADS = 32


def with_halo(cells, sides, width):
    for axis, dim in sides:
        count = lax.axis_size(axis)
        ends = count - 1
        head = lax.slice_in_dim(cells, 0, width, axis=dim)
        tail = lax.slice_in_dim(cells, cells.shape[dim] - width, cells.shape[dim], axis=dim)
        cells = jnp.concatenate(
            [
                lax.ppermute(tail, axis, [(i, (i + 1) % count) for i in range(ends)]),
                cells,
                lax.ppermute(head, axis, [((i + 1) % count, i) for i in range(ends)]),
            ],
            axis=dim,
        )
    return cells


def attend(head_qkv, head_size):
    nodes = head_qkv.shape[1]
    columns = head_qkv.shape[2]
    count_heads = columns // head_size
    query = head_qkv[0].reshape(nodes, count_heads, head_size)
    key = head_qkv[1].reshape(nodes, count_heads, head_size)
    value = head_qkv[2].reshape(nodes, count_heads, head_size)
    scale = 1.0 / head_size**0.5
    block = math.gcd(nodes, 512)

    def one_block(index):
        q_block = lax.dynamic_slice_in_dim(query, index * block, block, 0)
        score = jnp.einsum("qhc,khc->hqk", q_block, key, preferred_element_type=jnp.float32) * scale
        peak = jnp.max(score, -1, keepdims=True)
        expo = jnp.exp(score - peak)
        weight = (expo / jnp.sum(expo, -1, keepdims=True)).astype(jnp.bfloat16)
        result = jnp.einsum("hqk,khc->qhc", weight, value, preferred_element_type=jnp.float32)
        return result.astype(jnp.bfloat16).reshape(block, columns)

    blocks = lax.map(one_block, jnp.arange(nodes // block))
    return blocks.reshape(nodes, columns)


def message_term(mixed, w_mp):
    return jnp.dot(
        mixed, lax.all_gather(w_mp, "dom", axis=0, tiled=True), preferred_element_type=jnp.float32
    )


def body(feats, adj_own, adj_prev, adj_next, bcount, wqkv, w_mp, w_out):
    rows = feats.shape[0]
    width = feats.shape[1]
    band = adj_prev.shape[1]
    parts = lax.axis_size("dom")
    myself = lax.axis_index("dom")
    padded = with_halo(feats, (("dom", 0),), band)
    prev_rim = padded[:band]
    next_rim = padded[band + rows :]
    column = jnp.arange(band)
    prev_count = bcount[jnp.maximum(myself - 1, 0), 1]
    next_count = bcount[jnp.minimum(myself + 1, parts - 1), 0]
    prev_vis = (myself > 0) & (column >= band - prev_count)
    next_vis = (myself < parts - 1) & (column < next_count)
    own = adj_own.astype(jnp.bfloat16)
    prv = jnp.where(prev_vis[None, :], adj_prev, 0).astype(jnp.bfloat16)
    nxt = jnp.where(next_vis[None, :], adj_next, 0).astype(jnp.bfloat16)
    degree = (
        1.0
        + jnp.sum(own.astype(jnp.float32), -1)
        + jnp.sum(prv.astype(jnp.float32), -1)
        + jnp.sum(nxt.astype(jnp.float32), -1)
    )
    total = feats.astype(jnp.float32) + jnp.dot(own, feats, preferred_element_type=jnp.float32)
    total = total + jnp.dot(prv, prev_rim, preferred_element_type=jnp.float32)
    total = total + jnp.dot(nxt, next_rim, preferred_element_type=jnp.float32)
    mixed = (total / degree[:, None]).astype(jnp.bfloat16)
    node_qkv = jnp.einsum(
        "nd,tdc->tnc",
        feats,
        lax.all_gather(wqkv, "dom", axis=2, tiled=True),
        preferred_element_type=jnp.float32,
    ).astype(jnp.bfloat16)
    head_qkv = lax.all_to_all(node_qkv, "dom", split_axis=2, concat_axis=1, tiled=True)
    head_out = attend(head_qkv, width // HEADS)
    node_out = lax.all_to_all(head_out, "dom", split_axis=0, concat_axis=1, tiled=True)
    local = message_term(mixed, w_mp)
    attn = jnp.dot(
        node_out,
        lax.all_gather(w_out, "dom", axis=0, tiled=True),
        preferred_element_type=jnp.float32,
    )
    return (feats.astype(jnp.float32) + local + attn).astype(jnp.bfloat16)


def layer_kernel(
    parts, head_size,
    feats, adj_own, adj_prev, adj_next, bcount, wqkv, w_mp, w_out, out,
    fall, own_adj, prev_adj, next_adj, counts, wcat, w2, qs, kt, v1, ms, mr, lhs, keep,
    sib_out, sib_in, rs_out, rs_in, relay_in,
    load_sem, ag_send, ag_recv, mx_send, mx_recv, sb_send, sb_recv, rs_send, rs_recv,
):
    rows, width = feats.shape
    cols = w_out.shape[0]
    band = adj_prev.shape[0]
    half = rows // 2
    pair = 2 * rows
    heads = cols // head_size
    me = lax.axis_index("dom")
    core = me % 2
    chip = me // 2
    sib = me + 1 - 2 * core
    cx, cy = chip % 2, chip // 2

    def chip_at(dx, dy):
        return ((cy + dy) % 2) * 2 + (cx + dx) % 2

    x_chip, y_chip, d_chip = chip_at(1, 0), chip_at(0, 1), chip_at(1, 1)
    x_dev, y_dev, d_dev = x_chip * 2 + core, y_chip * 2 + core, d_chip * 2 + core
    mesh_id = pl.DeviceIdType.MESH

    def remote(src, dst, send_sem, recv_sem, dev):
        return pltpu.make_async_remote_copy(
            src_ref=src, dst_ref=dst, send_sem=send_sem, recv_sem=recv_sem,
            device_id={"dom": dev}, device_id_type=mesh_id,
        )

    pairs = [(feats, fall.at[me])]
    pairs += [(wqkv.at[t], wcat.at[:, pl.ds(t * cols, cols)]) for t in range(3)]
    pairs += [(adj_own, own_adj), (adj_prev, prev_adj), (adj_next, next_adj), (bcount, counts)]
    pairs += [(w_out, w2.at[pl.ds(0, cols)]), (w_mp, w2.at[pl.ds(cols, cols)])]
    loads = [pltpu.make_async_copy(a, b, load_sem.at[k]) for k, (a, b) in enumerate(pairs)]
    for load in loads:
        load.start()

    barrier = pltpu.get_barrier_semaphore()
    for k in range(1, parts):
        pl.semaphore_signal(barrier, inc=1, device_id={"dom": (me + k) % parts}, device_id_type=mesh_id)
    pl.semaphore_wait(barrier, parts - 1)

    started = []

    def send_half(block, h, dev, own=False):
        span = pl.ds(half * h, half)
        dst = fall.at[block, span]
        src = feats.at[span] if own else dst
        copy = remote(src, dst, ag_send.at[len(started)], ag_recv.at[block, h], dev)
        copy.start()
        started.append(copy)

    def wait_half(block, h):
        dst = fall.at[block, pl.ds(half * h, half)]
        remote(dst, dst, ag_send.at[0], ag_recv.at[block, h], sib).wait_recv()

    send_half(me, 0, x_dev, True)
    send_half(me, 1, y_dev, True)
    send_half(me, 0, sib, True)
    send_half(me, 1, sib, True)
    send_half(me, 1, x_dev, True)
    send_half(me, 0, y_dev, True)

    v1[:, cols:] = jnp.ones_like(v1[:, cols:])
    lane_head = lax.broadcasted_iota(jnp.int32, (1, cols), 1) // head_size
    factor = math.log2(math.e) / head_size**0.5

    def project(c):
        base = pl.multiple_of(c * pair, pair)
        block = fall[pl.ds(2 * c, 2)].reshape(pair, width)
        r = jnp.dot(block, wcat[...], preferred_element_type=jnp.float32)
        q = r[:, :cols] * factor
        for h in range(heads):
            qs[h, pl.ds(base, pair), :] = jnp.where(lane_head == h, q, 0.0).astype(jnp.bfloat16)
        kt[:, pl.ds(base, pair)] = r[:, cols : 2 * cols].T.astype(jnp.bfloat16)
        v1[pl.ds(base, pair), :cols] = r[:, 2 * cols :].astype(jnp.bfloat16)

    def wait_sib(c):
        for h in range(2):
            wait_half(2 * c + 1 - core, h)

    for load in loads:
        load.wait()
    wait_sib(chip)
    project(chip)
    wait_half(x_dev, 0)
    send_half(x_dev, 0, y_dev)
    send_half(x_dev, 0, sib)
    wait_half(y_dev, 1)
    send_half(y_dev, 1, x_dev)
    send_half(y_dev, 1, sib)
    wait_half(x_dev, 1)
    send_half(x_dev, 1, sib)
    wait_half(y_dev, 0)
    send_half(y_dev, 0, sib)
    wait_sib(x_chip)
    project(x_chip)
    wait_half(d_dev, 0)
    send_half(d_dev, 0, sib)
    wait_half(d_dev, 1)
    send_half(d_dev, 1, sib)
    wait_sib(y_chip)
    project(y_chip)
    wait_sib(d_chip)

    before, after = (me + parts - 1) % parts, (me + 1) % parts
    column = lax.broadcasted_iota(jnp.int32, (band, 1), 0)
    device = lax.broadcasted_iota(jnp.int32, (1, parts), 1)
    prev_count = jnp.sum(jnp.where((device == before) & (me > 0), counts[1:2], 0), -1, keepdims=True)
    next_count = jnp.sum(
        jnp.where((device == after) & (me < parts - 1), counts[0:1], 0), -1, keepdims=True
    )
    own = own_adj[...].astype(jnp.float32)
    prv = jnp.where(column >= band - prev_count, prev_adj[...], 0).astype(jnp.float32).T
    nxt = jnp.where(column < next_count, next_adj[...], 0).astype(jnp.float32).T
    degree = (
        1.0
        + jnp.sum(own, -1, keepdims=True)
        + jnp.sum(prv, -1, keepdims=True)
        + jnp.sum(nxt, -1, keepdims=True)
    )
    total = fall[me].astype(jnp.float32)
    total += jnp.dot(own.astype(jnp.bfloat16), fall[me], preferred_element_type=jnp.float32)
    total += jnp.dot(
        prv.astype(jnp.bfloat16), fall[before, rows - band :, :], preferred_element_type=jnp.float32
    )
    total += jnp.dot(
        nxt.astype(jnp.bfloat16), fall[after, :band, :], preferred_element_type=jnp.float32
    )
    mixed = (total / degree).astype(jnp.bfloat16)
    for j in range(parts):
        ms[j] = mixed[:, j * cols : (j + 1) * cols]
    mix_copies = []
    others = [2 * c + k for c in (d_chip, x_chip, y_chip) for k in (1 - core, core)] + [sib]
    for k, to in enumerate(others):
        copy = remote(ms.at[to], mr.at[me], mx_send.at[k], mx_recv.at[me], to)
        copy.start()
        mix_copies.append(copy)
    mr[me] = ms[me]
    project(d_chip)

    def attention(owner):
        base = pl.multiple_of(owner * rows, rows)
        result = jnp.zeros((rows, cols), jnp.float32)
        for h in range(heads):
            score = jnp.dot(
                qs[h, pl.ds(base, rows), :], kt[...], preferred_element_type=jnp.float32
            )
            peak = jnp.max(score, -1, keepdims=True)
            weight = jnp.exp2(score - peak).astype(jnp.bfloat16)
            both = jnp.dot(weight, v1[...], preferred_element_type=jnp.float32)
            result = jnp.where(lane_head == h, both[:, :cols] / both[:, cols:], result)
        lhs[:, :cols] = result.astype(jnp.bfloat16)

    def partial_sum(owner, arrives=True):
        attention(owner)
        if arrives:
            remote(mr.at[owner], mr.at[owner], mx_send.at[0], mx_recv.at[owner], sib).wait_recv()
        lhs[:, cols:] = mr[owner]
        return jnp.dot(lhs[...], w2[...], preferred_element_type=jnp.float32)

    def to_sib(slot):
        return remote(sib_out.at[slot], sib_in.at[slot], sb_send.at[slot], sb_recv.at[slot], sib)

    def unit(slot, c):
        sib_out[slot] = partial_sum(2 * c + 1 - core).astype(jnp.bfloat16)
        to_sib(slot).start()
        keep[slot] = partial_sum(2 * c + core, arrives=slot < 3)

    low, high = pl.ds(0, half), pl.ds(half, half)

    def combined(slot, span, extra=None):
        value = keep[slot, span] + sib_in[slot, span].astype(jnp.float32)
        if extra is not None:
            value += extra.astype(jnp.float32)
        rs_out[slot, span] = value.astype(jnp.bfloat16)

    x_relay = remote(rs_out.at[2, low], relay_in.at[0], rs_send.at[0], rs_recv.at[0], x_dev)
    y_relay = remote(rs_out.at[2, high], relay_in.at[1], rs_send.at[1], rs_recv.at[1], y_dev)
    x_low = remote(rs_out.at[0, low], rs_in.at[0, low], rs_send.at[2], rs_recv.at[2], x_dev)
    x_high = remote(rs_out.at[0, high], rs_in.at[0, high], rs_send.at[3], rs_recv.at[3], x_dev)
    y_low = remote(rs_out.at[1, low], rs_in.at[1, low], rs_send.at[4], rs_recv.at[4], y_dev)
    y_high = remote(rs_out.at[1, high], rs_in.at[1, high], rs_send.at[5], rs_recv.at[5], y_dev)

    unit(2, d_chip)
    to_sib(2).wait_recv()
    combined(2, low)
    x_relay.start()
    combined(2, high)
    y_relay.start()
    unit(0, x_chip)
    to_sib(0).wait_recv()
    combined(0, low)
    x_low.start()
    unit(1, y_chip)
    to_sib(1).wait_recv()
    combined(1, high)
    y_high.start()
    y_relay.wait_recv()
    combined(0, high, relay_in[1])
    x_high.start()
    x_relay.wait_recv()
    combined(1, low, relay_in[0])
    y_low.start()
    unit(3, chip)
    final = fall[me].astype(jnp.float32) + keep[3]
    to_sib(3).wait_recv()
    keep[3] = final + sib_in[3].astype(jnp.float32)
    x_low.wait_recv()
    y_high.wait_recv()
    x_high.wait_recv()
    y_low.wait_recv()
    out[...] = (
        keep[3] + rs_in[0].astype(jnp.float32) + rs_in[1].astype(jnp.float32)
    ).astype(out.dtype)
    for copy in started + mix_copies + [x_relay, y_relay, x_low, x_high, y_low, y_high]:
        copy.wait_send()
    for slot in range(4):
        to_sib(slot).wait_send()


def fused_layer(feats, adj_own, adj_prev, adj_next, bcount, wqkv, w_mp, w_out):
    rows, width = feats.shape
    cols = w_out.shape[0]
    parts = lax.axis_size("dom")
    nodes = rows * parts
    head_size = width // HEADS
    heads = cols // head_size
    vmem = pl.BlockSpec(memory_space=pltpu.VMEM)
    hbm = pl.BlockSpec(memory_space=pltpu.HBM)
    bf16, f32 = jnp.bfloat16, jnp.float32
    dma = pltpu.SemaphoreType.DMA
    return pl.pallas_call(
        functools.partial(layer_kernel, parts, head_size),
        out_shape=jax.ShapeDtypeStruct((rows, width), bf16),
        in_specs=[hbm] * 8,
        out_specs=vmem,
        scratch_shapes=[
            pltpu.VMEM((parts, rows, width), bf16),
            pltpu.VMEM(adj_own.shape, adj_own.dtype),
            pltpu.VMEM(adj_prev.shape[::-1], adj_prev.dtype),
            pltpu.VMEM(adj_next.shape[::-1], adj_next.dtype),
            pltpu.VMEM(bcount.shape[::-1], bcount.dtype),
            pltpu.VMEM((width, 3 * cols), bf16),
            pltpu.VMEM((2 * cols, width), bf16),
            pltpu.VMEM((heads, nodes, cols), bf16),
            pltpu.VMEM((cols, nodes), bf16),
            pltpu.VMEM((nodes, 2 * cols), bf16),
            pltpu.VMEM((parts, rows, cols), bf16),
            pltpu.VMEM((parts, rows, cols), bf16),
            pltpu.VMEM((rows, 2 * cols), bf16),
            pltpu.VMEM((4, rows, width), f32),
            pltpu.VMEM((4, rows, width), bf16),
            pltpu.VMEM((4, rows, width), bf16),
            pltpu.VMEM((3, rows, width), bf16),
            pltpu.VMEM((2, rows, width), bf16),
            pltpu.VMEM((2, rows // 2, width), bf16),
            dma((10,)),
            dma((14,)),
            dma((parts, 2)),
            dma((parts,)),
            dma((parts,)),
            dma((4,)),
            dma((4,)),
            dma((6,)),
            dma((6,)),
        ],
        compiler_params=pltpu.CompilerParams(
            collective_id=0, has_side_effects=True, vmem_limit_bytes=64 * 1024 * 1024
        ),
    )(feats, adj_own, adj_prev.T, adj_next.T, bcount.T, wqkv, w_mp, w_out)


def solution(mesh):
    placed = (
        P(("dp", "dom"), None),
        P(("dp", "dom"), None),
        P(("dp", "dom"), None),
        P(("dp", "dom"), None),
        P("dp", None),
        P(None, None, "dom"),
        P("dom", None),
        P("dom", None),
    )
    layer = fused_layer if mesh.shape["dom"] == 8 else body
    return jax.shard_map(
        layer, mesh=mesh, in_specs=placed, out_specs=P(("dp", "dom"), None), check_vma=False
    )
```

```python
import functools
import math

import jax
import jax.numpy as jnp
from jax import lax
from jax.experimental import pallas as pl
from jax.experimental.pallas import tpu as pltpu
from jax.sharding import PartitionSpec as P

HEADS = 32


def with_halo(cells, sides, width):
    for axis, dim in sides:
        count = lax.axis_size(axis)
        ends = count - 1
        head = lax.slice_in_dim(cells, 0, width, axis=dim)
        tail = lax.slice_in_dim(cells, cells.shape[dim] - width, cells.shape[dim], axis=dim)
        cells = jnp.concatenate(
            [
                lax.ppermute(tail, axis, [(i, (i + 1) % count) for i in range(ends)]),
                cells,
                lax.ppermute(head, axis, [((i + 1) % count, i) for i in range(ends)]),
            ],
            axis=dim,
        )
    return cells


def attend(head_qkv, head_size):
    nodes = head_qkv.shape[1]
    columns = head_qkv.shape[2]
    count_heads = columns // head_size
    query = head_qkv[0].reshape(nodes, count_heads, head_size)
    key = head_qkv[1].reshape(nodes, count_heads, head_size)
    value = head_qkv[2].reshape(nodes, count_heads, head_size)
    scale = 1.0 / head_size**0.5
    block = math.gcd(nodes, 512)

    def one_block(index):
        q_block = lax.dynamic_slice_in_dim(query, index * block, block, 0)
        score = jnp.einsum("qhc,khc->hqk", q_block, key, preferred_element_type=jnp.float32) * scale
        peak = jnp.max(score, -1, keepdims=True)
        expo = jnp.exp(score - peak)
        weight = (expo / jnp.sum(expo, -1, keepdims=True)).astype(jnp.bfloat16)
        result = jnp.einsum("hqk,khc->qhc", weight, value, preferred_element_type=jnp.float32)
        return result.astype(jnp.bfloat16).reshape(block, columns)

    blocks = lax.map(one_block, jnp.arange(nodes // block))
    return blocks.reshape(nodes, columns)


def message_term(mixed, w_mp):
    return jnp.dot(
        mixed, lax.all_gather(w_mp, "dom", axis=0, tiled=True), preferred_element_type=jnp.float32
    )


def body(feats, adj_own, adj_prev, adj_next, bcount, wqkv, w_mp, w_out):
    rows = feats.shape[0]
    width = feats.shape[1]
    band = adj_prev.shape[1]
    parts = lax.axis_size("dom")
    myself = lax.axis_index("dom")
    padded = with_halo(feats, (("dom", 0),), band)
    prev_rim = padded[:band]
    next_rim = padded[band + rows :]
    column = jnp.arange(band)
    prev_count = bcount[jnp.maximum(myself - 1, 0), 1]
    next_count = bcount[jnp.minimum(myself + 1, parts - 1), 0]
    prev_vis = (myself > 0) & (column >= band - prev_count)
    next_vis = (myself < parts - 1) & (column < next_count)
    own = adj_own.astype(jnp.bfloat16)
    prv = jnp.where(prev_vis[None, :], adj_prev, 0).astype(jnp.bfloat16)
    nxt = jnp.where(next_vis[None, :], adj_next, 0).astype(jnp.bfloat16)
    degree = (
        1.0
        + jnp.sum(own.astype(jnp.float32), -1)
        + jnp.sum(prv.astype(jnp.float32), -1)
        + jnp.sum(nxt.astype(jnp.float32), -1)
    )
    total = feats.astype(jnp.float32) + jnp.dot(own, feats, preferred_element_type=jnp.float32)
    total = total + jnp.dot(prv, prev_rim, preferred_element_type=jnp.float32)
    total = total + jnp.dot(nxt, next_rim, preferred_element_type=jnp.float32)
    mixed = (total / degree[:, None]).astype(jnp.bfloat16)
    node_qkv = jnp.einsum(
        "nd,tdc->tnc",
        feats,
        lax.all_gather(wqkv, "dom", axis=2, tiled=True),
        preferred_element_type=jnp.float32,
    ).astype(jnp.bfloat16)
    head_qkv = lax.all_to_all(node_qkv, "dom", split_axis=2, concat_axis=1, tiled=True)
    head_out = attend(head_qkv, width // HEADS)
    node_out = lax.all_to_all(head_out, "dom", split_axis=0, concat_axis=1, tiled=True)
    local = message_term(mixed, w_mp)
    attn = jnp.dot(
        node_out,
        lax.all_gather(w_out, "dom", axis=0, tiled=True),
        preferred_element_type=jnp.float32,
    )
    return (feats.astype(jnp.float32) + local + attn).astype(jnp.bfloat16)


def layer_kernel(
    parts, head_size,
    feats, adj_own, adj_prev, adj_next, bcount, wqkv, w_mp, w_out, out,
    fall, own_adj, prev_adj, next_adj, counts, wcat, w2, qs, kt, v1, ms, mr, lhs, keep,
    sib_out, sib_in, rs_out, rs_in, relay_in,
    load_sem, ag_send, ag_recv, mx_send, mx_recv, sb_send, sb_recv, rs_send, rs_recv,
):
    rows, width = feats.shape
    cols = w_out.shape[0]
    band = adj_prev.shape[0]
    half = rows // 2
    pair = 2 * rows
    heads = cols // head_size
    me = lax.axis_index("dom")
    core = me % 2
    chip = me // 2
    sib = me + 1 - 2 * core
    cx, cy = chip % 2, chip // 2

    def chip_at(dx, dy):
        return ((cy + dy) % 2) * 2 + (cx + dx) % 2

    x_chip, y_chip, d_chip = chip_at(1, 0), chip_at(0, 1), chip_at(1, 1)
    x_dev, y_dev, d_dev = x_chip * 2 + core, y_chip * 2 + core, d_chip * 2 + core
    mesh_id = pl.DeviceIdType.MESH

    def remote(src, dst, send_sem, recv_sem, dev):
        return pltpu.make_async_remote_copy(
            src_ref=src, dst_ref=dst, send_sem=send_sem, recv_sem=recv_sem,
            device_id={"dom": dev}, device_id_type=mesh_id,
        )

    pairs = [(feats, fall.at[me])]
    pairs += [(wqkv.at[t], wcat.at[:, pl.ds(t * cols, cols)]) for t in range(3)]
    pairs += [(adj_own, own_adj), (adj_prev, prev_adj), (adj_next, next_adj), (bcount, counts)]
    pairs += [(w_out, w2.at[pl.ds(0, cols)]), (w_mp, w2.at[pl.ds(cols, cols)])]
    loads = [pltpu.make_async_copy(a, b, load_sem.at[k]) for k, (a, b) in enumerate(pairs)]
    for load in loads:
        load.start()

    barrier = pltpu.get_barrier_semaphore()
    for k in range(1, parts):
        pl.semaphore_signal(barrier, inc=1, device_id={"dom": (me + k) % parts}, device_id_type=mesh_id)
    pl.semaphore_wait(barrier, parts - 1)

    started = []

    def send_half(block, h, dev, own=False):
        span = pl.ds(half * h, half)
        dst = fall.at[block, span]
        src = feats.at[span] if own else dst
        copy = remote(src, dst, ag_send.at[len(started)], ag_recv.at[block, h], dev)
        copy.start()
        started.append(copy)

    def wait_half(block, h):
        dst = fall.at[block, pl.ds(half * h, half)]
        remote(dst, dst, ag_send.at[0], ag_recv.at[block, h], sib).wait_recv()

    send_half(me, 0, x_dev, True)
    send_half(me, 1, y_dev, True)
    send_half(me, 0, sib, True)
    send_half(me, 1, sib, True)
    send_half(me, 1, x_dev, True)
    send_half(me, 0, y_dev, True)

    v1[:, cols:] = jnp.ones_like(v1[:, cols:])
    lane_head = lax.broadcasted_iota(jnp.int32, (1, cols), 1) // head_size
    factor = math.log2(math.e) / head_size**0.5

    def project(c):
        base = pl.multiple_of(c * pair, pair)
        block = fall[pl.ds(2 * c, 2)].reshape(pair, width)
        r = jnp.dot(block, wcat[...], preferred_element_type=jnp.float32)
        q = r[:, :cols] * factor
        for h in range(heads):
            qs[h, pl.ds(base, pair), :] = jnp.where(lane_head == h, q, 0.0).astype(jnp.bfloat16)
        kt[:, pl.ds(base, pair)] = r[:, cols : 2 * cols].T.astype(jnp.bfloat16)
        v1[pl.ds(base, pair), :cols] = r[:, 2 * cols :].astype(jnp.bfloat16)

    def wait_sib(c):
        for h in range(2):
            wait_half(2 * c + 1 - core, h)

    for load in loads:
        load.wait()
    wait_sib(chip)
    project(chip)
    before, after = (me + parts - 1) % parts, (me + 1) % parts
    column = lax.broadcasted_iota(jnp.int32, (band, 1), 0)
    device = lax.broadcasted_iota(jnp.int32, (1, parts), 1)
    prev_count = jnp.sum(jnp.where((device == before) & (me > 0), counts[1:2], 0), -1, keepdims=True)
    next_count = jnp.sum(
        jnp.where((device == after) & (me < parts - 1), counts[0:1], 0), -1, keepdims=True
    )
    own = own_adj[...].astype(jnp.float32)
    prv = jnp.where(column >= band - prev_count, prev_adj[...], 0).astype(jnp.float32).T
    nxt = jnp.where(column < next_count, next_adj[...], 0).astype(jnp.float32).T
    degree = (
        1.0
        + jnp.sum(own, -1, keepdims=True)
        + jnp.sum(prv, -1, keepdims=True)
        + jnp.sum(nxt, -1, keepdims=True)
    )
    total = fall[me].astype(jnp.float32)
    total += jnp.dot(own.astype(jnp.bfloat16), fall[me], preferred_element_type=jnp.float32)
    wait_half(x_dev, 0)
    send_half(x_dev, 0, y_dev)
    send_half(x_dev, 0, sib)
    wait_half(y_dev, 1)
    send_half(y_dev, 1, x_dev)
    send_half(y_dev, 1, sib)
    wait_half(x_dev, 1)
    send_half(x_dev, 1, sib)
    wait_half(y_dev, 0)
    send_half(y_dev, 0, sib)
    wait_sib(x_chip)
    project(x_chip)
    wait_half(d_dev, 0)
    send_half(d_dev, 0, sib)
    wait_half(d_dev, 1)
    send_half(d_dev, 1, sib)
    wait_sib(y_chip)
    project(y_chip)
    wait_sib(d_chip)

    total += jnp.dot(
        prv.astype(jnp.bfloat16), fall[before, rows - band :, :], preferred_element_type=jnp.float32
    )
    total += jnp.dot(
        nxt.astype(jnp.bfloat16), fall[after, :band, :], preferred_element_type=jnp.float32
    )
    mixed = (total / degree).astype(jnp.bfloat16)
    for j in range(parts):
        ms[j] = mixed[:, j * cols : (j + 1) * cols]
    mix_copies = []
    others = [2 * c + k for c in (d_chip, x_chip, y_chip) for k in (1 - core, core)] + [sib]
    for k, to in enumerate(others):
        copy = remote(ms.at[to], mr.at[me], mx_send.at[k], mx_recv.at[me], to)
        copy.start()
        mix_copies.append(copy)
    mr[me] = ms[me]
    project(d_chip)

    def attention(owner):
        base = pl.multiple_of(owner * rows, rows)
        top = jnp.zeros((rows, cols), jnp.float32)
        bottom = jnp.ones((rows, cols), jnp.float32)
        for h in range(heads):
            score = jnp.dot(
                qs[h, pl.ds(base, rows), :], kt[...], preferred_element_type=jnp.float32
            )
            peak = jnp.max(score, -1, keepdims=True)
            weight = jnp.exp2(score - peak).astype(jnp.bfloat16)
            both = jnp.dot(weight, v1[...], preferred_element_type=jnp.float32)
            top = jnp.where(lane_head == h, both[:, :cols], top)
            bottom = jnp.where(lane_head == h, both[:, cols:], bottom)
        lhs[:, :cols] = (top / bottom).astype(jnp.bfloat16)

    def partial_sum(owner, arrives=True):
        attention(owner)
        if arrives:
            remote(mr.at[owner], mr.at[owner], mx_send.at[0], mx_recv.at[owner], sib).wait_recv()
        lhs[:, cols:] = mr[owner]
        return jnp.dot(lhs[...], w2[...], preferred_element_type=jnp.float32)

    def to_sib(slot):
        return remote(sib_out.at[slot], sib_in.at[slot], sb_send.at[slot], sb_recv.at[slot], sib)

    def unit(slot, c):
        sib_out[slot] = partial_sum(2 * c + 1 - core).astype(jnp.bfloat16)
        to_sib(slot).start()
        keep[slot] = partial_sum(2 * c + core, arrives=slot < 3)

    low, high = pl.ds(0, half), pl.ds(half, half)

    def combined(slot, span, extra=None):
        value = keep[slot, span] + sib_in[slot, span].astype(jnp.float32)
        if extra is not None:
            value += extra.astype(jnp.float32)
        rs_out[slot, span] = value.astype(jnp.bfloat16)

    x_relay = remote(rs_out.at[2, low], relay_in.at[0], rs_send.at[0], rs_recv.at[0], x_dev)
    y_relay = remote(rs_out.at[2, high], relay_in.at[1], rs_send.at[1], rs_recv.at[1], y_dev)
    x_low = remote(rs_out.at[0, low], rs_in.at[0, low], rs_send.at[2], rs_recv.at[2], x_dev)
    x_high = remote(rs_out.at[0, high], rs_in.at[0, high], rs_send.at[3], rs_recv.at[3], x_dev)
    y_low = remote(rs_out.at[1, low], rs_in.at[1, low], rs_send.at[4], rs_recv.at[4], y_dev)
    y_high = remote(rs_out.at[1, high], rs_in.at[1, high], rs_send.at[5], rs_recv.at[5], y_dev)

    unit(2, d_chip)
    to_sib(2).wait_recv()
    combined(2, low)
    x_relay.start()
    combined(2, high)
    y_relay.start()
    unit(0, x_chip)
    to_sib(0).wait_recv()
    combined(0, low)
    x_low.start()
    unit(1, y_chip)
    to_sib(1).wait_recv()
    combined(1, high)
    y_high.start()
    y_relay.wait_recv()
    combined(0, high, relay_in[1])
    x_high.start()
    x_relay.wait_recv()
    combined(1, low, relay_in[0])
    y_low.start()
    unit(3, chip)
    final = fall[me].astype(jnp.float32) + keep[3]
    to_sib(3).wait_recv()
    keep[3] = final + sib_in[3].astype(jnp.float32)
    x_low.wait_recv()
    y_high.wait_recv()
    x_high.wait_recv()
    y_low.wait_recv()
    out[...] = (
        keep[3] + rs_in[0].astype(jnp.float32) + rs_in[1].astype(jnp.float32)
    ).astype(out.dtype)
    for copy in started + mix_copies + [x_relay, y_relay, x_low, x_high, y_low, y_high]:
        copy.wait_send()
    for slot in range(4):
        to_sib(slot).wait_send()


def fused_layer(feats, adj_own, adj_prev, adj_next, bcount, wqkv, w_mp, w_out):
    rows, width = feats.shape
    cols = w_out.shape[0]
    parts = lax.axis_size("dom")
    nodes = rows * parts
    head_size = width // HEADS
    heads = cols // head_size
    vmem = pl.BlockSpec(memory_space=pltpu.VMEM)
    hbm = pl.BlockSpec(memory_space=pltpu.HBM)
    bf16, f32 = jnp.bfloat16, jnp.float32
    dma = pltpu.SemaphoreType.DMA
    return pl.pallas_call(
        functools.partial(layer_kernel, parts, head_size),
        out_shape=jax.ShapeDtypeStruct((rows, width), bf16),
        in_specs=[hbm] * 8,
        out_specs=vmem,
        scratch_shapes=[
            pltpu.VMEM((parts, rows, width), bf16),
            pltpu.VMEM(adj_own.shape, adj_own.dtype),
            pltpu.VMEM(adj_prev.shape[::-1], adj_prev.dtype),
            pltpu.VMEM(adj_next.shape[::-1], adj_next.dtype),
            pltpu.VMEM(bcount.shape[::-1], bcount.dtype),
            pltpu.VMEM((width, 3 * cols), bf16),
            pltpu.VMEM((2 * cols, width), bf16),
            pltpu.VMEM((heads, nodes, cols), bf16),
            pltpu.VMEM((cols, nodes), bf16),
            pltpu.VMEM((nodes, 2 * cols), bf16),
            pltpu.VMEM((parts, rows, cols), bf16),
            pltpu.VMEM((parts, rows, cols), bf16),
            pltpu.VMEM((rows, 2 * cols), bf16),
            pltpu.VMEM((4, rows, width), f32),
            pltpu.VMEM((4, rows, width), bf16),
            pltpu.VMEM((4, rows, width), bf16),
            pltpu.VMEM((3, rows, width), bf16),
            pltpu.VMEM((2, rows, width), bf16),
            pltpu.VMEM((2, rows // 2, width), bf16),
            dma((10,)),
            dma((14,)),
            dma((parts, 2)),
            dma((parts,)),
            dma((parts,)),
            dma((4,)),
            dma((4,)),
            dma((6,)),
            dma((6,)),
        ],
        compiler_params=pltpu.CompilerParams(
            collective_id=0, has_side_effects=True, vmem_limit_bytes=64 * 1024 * 1024
        ),
    )(feats, adj_own, adj_prev.T, adj_next.T, bcount.T, wqkv, w_mp, w_out)


def solution(mesh):
    placed = (
        P(("dp", "dom"), None),
        P(("dp", "dom"), None),
        P(("dp", "dom"), None),
        P(("dp", "dom"), None),
        P("dp", None),
        P(None, None, "dom"),
        P("dom", None),
        P("dom", None),
    )
    layer = fused_layer if mesh.shape["dom"] == 8 else body
    return jax.shard_map(
        layer, mesh=mesh, in_specs=placed, out_specs=P(("dp", "dom"), None), check_vma=False
    )
```
